1024 devices in a mesh: dom: 64 (over z, core), sub: 16 (over y, x).
Axes of the slice: x: 4, y: 4, z: 32, core: 2. Of those that a mesh axis runs over, the one named last changes fastest.
Arguments:
- coupling: bfloat16 [8192, 6, 128, 128], P(('dom', 'sub')), may hold values from -0.25 to 0.25
- diag_inv: bfloat16 [8192, 128, 128], P(('dom', 'sub')), may hold values from -0.5 to 0.5
- rhs: float32 [8192, 64, 128], P(('dom', 'sub')), may hold values from -6 to 6
- color: int32 [8192], P(('dom', 'sub')), may hold values from 0 to 3, as said below
- local_target: int32 [8192, 2], P(('dom', 'sub')), may hold values from 0 to 7, as said below
- group_peer: int32 [8192, 2], P(('dom', 'sub')), may hold values from 0 to 15, as said below
- group_list: int32 [1024, 4, 16], P(('dom', 'sub')), may hold values from -1 to 7, as said below
- dom_target: int32 [8192, 2], P(('dom', 'sub')), may hold values from 0 to 7, as said below
Outputs:
- solution: float32 [8192, 64, 128], P(('dom', 'sub'))
- defect: float32 [8192, 64, 128], P(('dom', 'sub'))
The draws below stay inside these ranges and needn't reach their ends.
Inputs may be any that keep to these rules, and one draw needn't show every extreme that they name: Each partition window of 8 consecutive block rows holds exactly a quarter of its rows of each color. `local_target`: A row of another color than row i, in the same partition window. `group_peer`: never the row's own member of the group; the two entries of a row differ. `group_list`: entry [p, c, q] is the local index on member q of p's group of a row of another color than c that receives all of p's color-c couplings to q, and -1 where p has none; a partition sends at most one row's sum to each member in a color. `dom_target`: groups form a cycle; the row reached is always of another color than row i.
All inputs are finite; a program needn't handle non-finite values.
Results may differ from the reference program's by a relative error of at most 0.012.
Values sent between devices are 32-bit elements; how exact they have to be, the bound alone decides.
A program may use at most 32 MiB of HBM per device.

```python
import jax
import jax.numpy as jnp
from jax import lax

B = 128
NRHS = 64
ROWS_DEV = 8
COLORS = 4
SWEEPS = 2
COUPLINGS = 6
GROUP = 16
NPART = 1024
NROWS = 8192


def pattern(base_key):
    quarter = ROWS_DEV // 4
    groups = NPART // GROUP
    subkeys = jax.random.split(base_key, 8)
    scores = jax.random.randint(subkeys[0], (NPART, ROWS_DEV), 0, 1 << 20) * ROWS_DEV + jnp.arange(ROWS_DEV, dtype=jnp.int32)[None, :]
    shuffle = jnp.argsort(scores, axis=1).astype(jnp.int32)
    inverse = jnp.argsort(shuffle, axis=1).astype(jnp.int32)
    row_color = (shuffle // quarter).astype(jnp.int32)
    rows_of = inverse.reshape(NPART, 4, quarter)

    def pick(seed_key, part_index, avoid):
        first_key, second_key = jax.random.split(seed_key)
        other_color = (avoid + jax.random.randint(first_key, avoid.shape, 1, 4)) % 4
        position = jax.random.randint(second_key, avoid.shape, 0, quarter)
        part_full = jnp.broadcast_to(part_index, avoid.shape)
        return rows_of[part_full, other_color, position].astype(jnp.int32)
    part_ids = jnp.arange(NPART, dtype=jnp.int32)[:, None]
    group_of = part_ids // GROUP
    member = part_ids % GROUP
    local_rows = pick(subkeys[1], part_ids[:, :, None], jnp.broadcast_to(row_color[:, :, None], (NPART, ROWS_DEV, 2)))
    up_part = (group_of + 1) % groups * GROUP + member
    down_part = (group_of - 1 + groups) % groups * GROUP + member
    up_rows = pick(subkeys[2], up_part, row_color)
    down_rows = pick(subkeys[3], down_part, row_color)
    dom_rows = jnp.stack([up_rows, down_rows], axis=-1)
    busiest = jax.random.randint(subkeys[4], (groups, 4), 0, GROUP)
    busiest_row = busiest[jnp.broadcast_to(group_of, (NPART, ROWS_DEV)), row_color]
    first_off = jax.random.randint(subkeys[5], (NPART, ROWS_DEV), 1, GROUP)
    leading = shuffle % quarter == 0
    forced = (busiest_row - member) % GROUP
    first_off = jnp.where(leading & (forced != 0), forced, first_off)
    second_off = 1 + (first_off - 1 + jax.random.randint(subkeys[6], (NPART, ROWS_DEV), 1, GROUP - 1)) % (GROUP - 1)
    peer_ids = ((member[:, :, None] + jnp.stack([first_off, second_off], axis=-1)) % GROUP).astype(jnp.int32)
    color_ids = jnp.arange(4, dtype=jnp.int32)
    members = jnp.arange(GROUP, dtype=jnp.int32)
    in_use = jnp.any((row_color[:, :, None, None, None] == color_ids[None, None, None, :, None]) & (peer_ids[:, :, :, None, None] == members[None, None, None, None, :]), axis=(1, 2))
    dest_part = jnp.broadcast_to((group_of * GROUP + members[None, :])[:, None, :], (NPART, 4, GROUP))
    dest_rows = pick(subkeys[7], dest_part, jnp.broadcast_to(color_ids[None, :, None], (NPART, 4, GROUP)))
    send_list = jnp.where(in_use, dest_rows, -1).astype(jnp.int32)
    return (row_color.reshape(-1), local_rows.reshape(-1, 2), peer_ids.reshape(-1, 2), send_list, dom_rows.reshape(-1, 2))


def draw_color(key, part):
    return pattern(jax.random.fold_in(key, 4021))[0]


def draw_local_target(key, part):
    return pattern(jax.random.fold_in(key, 4021))[1]


def draw_group_peer(key, part):
    return pattern(jax.random.fold_in(key, 4021))[2]


def draw_group_list(key, part):
    return pattern(jax.random.fold_in(key, 4021))[3]


def draw_dom_target(key, part):
    return pattern(jax.random.fold_in(key, 4021))[4]


def block_levels(own_key, dims, cuts, least, high):
    level, own = 1.0, jax.random.fold_in(own_key, 6)
    for dim, blocks in cuts:
        steps = jnp.exp(jax.random.uniform(jax.random.fold_in(own, dim), (blocks,), jnp.float32, least / len(cuts), high / len(cuts)))
        level = level * jnp.repeat(steps, dims[dim] // blocks).reshape([-1 if axis == dim else 1 for axis in range(len(dims))])
    return level


def bell_draw(key, dims, width, most, cuts=(), kind=jnp.bfloat16):
    factor_of = block_levels(key, dims, cuts, -0.22, 0.18) if cuts else 1.0
    result = jax.random.normal(key, dims, jnp.float32) * width * factor_of
    return jnp.minimum(jnp.maximum(result, -most), most).astype(kind)


def setup_inputs(seed: int = 0) -> dict:
    seeds = jax.random.split(jax.random.key(seed), 9)
    return {
        "coupling": bell_draw(seeds[0], (NROWS, COUPLINGS, B, B), (4 * B) ** -0.5, 0.25, ((0, 1024),)),
        "diag_inv": bell_draw(seeds[1], (NROWS, B, B), B ** -0.5, 0.5, ((0, 1024),)),
        "rhs": bell_draw(seeds[2], (NROWS, NRHS, B), 1.0, 6.0, ((0, 1024),), jnp.float32),
        "color": draw_color(jax.random.fold_in(seeds[8], 71), 0),
        "local_target": draw_local_target(jax.random.fold_in(seeds[8], 71), 0),
        "group_peer": draw_group_peer(jax.random.fold_in(seeds[8], 71), 0),
        "group_list": draw_group_list(jax.random.fold_in(seeds[8], 71), 0),
        "dom_target": draw_dom_target(jax.random.fold_in(seeds[8], 71), 0),
    }


def reference(coupling, diag_inv, rhs, color, local_target, group_peer, group_list, dom_target):
    row_count = rhs.shape[0]
    row_index = jnp.arange(row_count, dtype=jnp.int32)
    partition = row_index // ROWS_DEV
    group_of = partition // GROUP
    member = partition % GROUP
    groups = NPART // GROUP
    local_rows = partition[:, None] * ROWS_DEV + local_target
    peer_rows = group_list[partition[:, None], color[:, None], group_peer]
    group_rows = (group_of[:, None] * GROUP + group_peer) * ROWS_DEV + peer_rows
    up_rows = (((group_of + 1) % groups) * GROUP + member) * ROWS_DEV + dom_target[:, 0]
    down_rows = (((group_of - 1 + groups) % groups) * GROUP + member) * ROWS_DEV + dom_target[:, 1]
    targets = jnp.concatenate([local_rows, group_rows, up_rows[:, None], down_rows[:, None]], axis=1).astype(jnp.int32)
    by_color = jnp.argsort(color, stable=True).astype(jnp.int32).reshape(COLORS, row_count // COLORS)
    solution = jnp.zeros(rhs.shape, jnp.float32)
    coupled = jnp.zeros(rhs.shape, jnp.float32)
    for sweep_no in range(SWEEPS):
        for color_now in range(COLORS):
            picked = by_color[color_now]
            update_in = (rhs[picked] - coupled[picked]).astype(jnp.bfloat16)
            updated = jnp.einsum("prb,pbe->pre", update_in.astype(jnp.float32), diag_inv[picked].astype(jnp.float32), precision=lax.Precision.HIGHEST)
            change = (updated - solution[picked]).astype(jnp.bfloat16)
            solution = solution.at[picked].set(updated)
            products = jnp.einsum("prb,pkbe->pkre", change.astype(jnp.float32), coupling[picked].astype(jnp.float32), precision=lax.Precision.HIGHEST)
            flat_products = products.reshape(-1, rhs.shape[1], rhs.shape[2])
            coupled = coupled + jax.ops.segment_sum(flat_products, targets[picked].reshape(-1), num_segments=row_count)
    return solution, rhs - coupled
```

```python
import functools

import jax
import jax.numpy as jnp
from jax import lax
from jax.experimental import pallas as pl
from jax.experimental.pallas import tpu as pltpu
from jax.sharding import PartitionSpec as P

MESH = pl.DeviceIdType.MESH
COLORS = 4
SWEEPS = 2
STEPS = COLORS * SWEEPS
SIDE = 4
OFFSETS = sorted(
    [(dx, dy) for dy in range(SIDE) for dx in range(SIDE) if (dx, dy) != (0, 0)],
    key=lambda o: -(min(o[0], SIDE - o[0]) + min(o[1], SIDE - o[1])),
)
PEERS = len(OFFSETS)
STREAMS = 2


def kernel(
    parts, group, coup, diag, rhs, color, ltgt, gpeer, glist, dtgt, sol_out, def_out,
    recv, drecv, send, dsend, tag_send, tag_recv, resid, solb, near, jrow, rank,
    rsem, ssem, tag_rsem, tag_ssem,
):
    me = lax.axis_index("sub")
    dom = lax.axis_index("dom")
    me_x, me_y = me % SIDE, me // SIDE
    peers = [((me_y + dy) % SIDE) * SIDE + (me_x + dx) % SIDE for dx, dy in OFFSETS]
    above, below = (dom + 1) % group, (dom + group - 1) % group
    devices = [{"sub": q} for q in peers] + [{"dom": above}, {"dom": below}]
    rows_dev, rhs_count, width = rhs.shape
    rows = rhs_count // parts

    barrier = pltpu.get_barrier_semaphore()
    for d in devices:
        pl.semaphore_signal(barrier, inc=1, device_id=d, device_id_type=MESH)

    colors = [color[r] for r in range(rows_dev)]
    slots = []
    for c in range(COLORS):
        first, total = jnp.int32(rows_dev - 1), jnp.int32(0)
        for r in reversed(range(rows_dev)):
            hit = colors[r] == c
            first = jnp.where(hit, r, first)
            total = total + jnp.where(hit, r, 0)
        slots += [first, jnp.clip(total - first, 0, rows_dev - 1)]
    for s, j in enumerate(slots):
        jrow[s] = j
    for r in range(rows_dev):
        place = jnp.int32(0)
        for s, j in enumerate(slots):
            place = jnp.where(j == r, s, place)
        rank[r] = place
    for s, j in enumerate(slots):
        resid[s] = rhs[j]
    solb[...] = jnp.zeros_like(solb)

    line = lax.broadcasted_iota(jnp.int32, (8, width), 0)
    for n, q in enumerate(peers):
        tile = jnp.full((8, width), -1, jnp.int32)
        for c in range(COLORS):
            tile = jnp.where(line == c, glist[0, c, q], tile)
        tag_send[n] = tile
    for way in range(2):
        tile = jnp.full((8, width), -1, jnp.int32)
        for s, j in enumerate(slots):
            tile = jnp.where(line == s, dtgt[j, way], tile)
        tag_send[PEERS + way] = tile

    def tag_copy(n):
        return pltpu.make_async_remote_copy(
            src_ref=tag_send.at[n], dst_ref=tag_recv.at[n], send_sem=tag_ssem.at[n],
            recv_sem=tag_rsem.at[n], device_id=devices[n], device_id_type=MESH,
        )

    def copy(t, n, part):
        if n < PEERS:
            src, dst = send.at[t % 2, n, part], recv.at[t, n, part]
        else:
            src, dst = dsend.at[t % 2, n - PEERS, part], drecv.at[t, n - PEERS, part]
        return pltpu.make_async_remote_copy(
            src_ref=src, dst_ref=dst, send_sem=ssem.at[t % 2, n, part],
            recv_sem=rsem.at[t % 2, n, part], device_id=devices[n], device_id_type=MESH,
        )

    def gather(t, part, into):
        c = t % COLORS
        span = pl.ds(part * rows, rows)
        targets = [jrow[s] for s in into]
        totals = [resid[s, span, :] for s in into]
        for n in range(PEERS):
            tag = jnp.broadcast_to(tag_recv[n, pl.ds(c, 1), :], (rows, width))
            item = recv[t, n, part]
            totals = [x - jnp.where(tag == j, item, 0.0) for x, j in zip(totals, targets)]
        for way in range(2):
            for i in range(2):
                tag = jnp.broadcast_to(tag_recv[PEERS + way, pl.ds(2 * c + i, 1), :], (rows, width))
                item = drecv[t, way, part, i]
                totals = [x - jnp.where(tag == j, item, 0.0) for x, j in zip(totals, targets)]
        for s, x in zip(into, totals):
            resid[s, span, :] = x

    def pair(c):
        return [2 * (c % COLORS), 2 * (c % COLORS) + 1]

    def solve(t, part, first):
        c = t % COLORS
        span = pl.ds(part * rows, rows)
        if not first:
            for n in range(PEERS + 2):
                copy(t - 1, n, part).wait_recv()
            gather(t - 1, part, pair(c))
        changes = []
        for s in pair(c):
            new = jnp.dot(
                resid[s, span, :].astype(jnp.bfloat16), diag[jrow[s]], preferred_element_type=jnp.float32
            )
            changes.append((new - solb[s, span, :]).astype(jnp.bfloat16))
            solb[s, span, :] = new
        owners = [jrow[s] for s in pair(c)]

        def products(i, k):
            both = jnp.concatenate([coup[owners[i], k], coup[owners[i], k + 1]], axis=1)
            out = jnp.dot(changes[i], both, preferred_element_type=jnp.float32)
            return out[:, :width], out[:, width:]

        terms = [products(i, 2) for i in range(2)]
        wants = [[jnp.full((rows, width), gpeer[j, k], jnp.int32) for k in range(2)] for j in owners]
        for n, q in enumerate(peers):
            sums = [
                jnp.where(want[0] == q, term[0], jnp.where(want[1] == q, term[1], 0.0))
                for want, term in zip(wants, terms)
            ]
            send[t % 2, n, part] = sums[0] + sums[1]
        for i in range(2):
            up, down = products(i, 4)
            dsend[t % 2, 0, part, i] = up
            dsend[t % 2, 1, part, i] = down
        for i in range(2):
            near[part, i, 0], near[part, i, 1] = products(i, 0)

    def launch(t, part):
        for n in range(PEERS + 2):
            copy(t, n, part).start()

    def local(t, part):
        c = t % COLORS
        span = pl.ds(part * rows, rows)
        into = pair(c + 1) + pair(c + 2) + pair(c + 3)
        targets = [jrow[s] for s in into]
        totals = [resid[s, span, :] for s in into]
        for i, s in enumerate(pair(c)):
            for k in range(2):
                tag = jnp.full((rows, width), ltgt[jrow[s], k], jnp.int32)
                item = near[part, i, k]
                totals = [x - jnp.where(tag == j, item, 0.0) for x, j in zip(totals, targets)]
        for s, x in zip(into, totals):
            resid[s, span, :] = x

    for part in range(parts):
        solve(0, part, True)
    pl.semaphore_wait(barrier, PEERS + 2)
    for n in range(PEERS + 2):
        tag_copy(n).start()
    for part in range(parts):
        launch(0, part)
    for part in range(parts):
        local(0, part)
    for n in range(PEERS + 2):
        tag_copy(n).wait_recv()

    def step(t, carry):
        for part in range(parts):
            @pl.when(t >= 2)
            def _():
                for n in range(PEERS + 2):
                    copy(t, n, part).wait_send()

            solve(t, part, False)
            launch(t, part)
            local(t, part)
            gather(t - 1, part, pair(t + 1) + pair(t + 2))
        return carry

    lax.fori_loop(1, STEPS, step, 0)
    for r in range(rows_dev):
        sol_out[r] = solb[rank[r]]
    last = STEPS - 1
    for part in range(parts):
        for n in range(PEERS + 2):
            copy(last, n, part).wait_recv()
        gather(last, part, pair(0) + pair(1) + pair(2))
    for r in range(rows_dev):
        def_out[r] = resid[rank[r]]
    for part in range(parts):
        for n in range(PEERS + 2):
            copy(last - 1, n, part).wait_send()
            copy(last, n, part).wait_send()
    for n in range(PEERS + 2):
        tag_copy(n).wait_send()


def on_device(coupling, diag_inv, rhs, color, local_target, group_peer, group_list, dom_target):
    rows_dev, rhs_count, width = rhs.shape
    parts, rows = STREAMS, rhs_count // STREAMS
    vmem, smem = pl.BlockSpec(memory_space=pltpu.VMEM), pl.BlockSpec(memory_space=pltpu.SMEM)
    ends = PEERS + 2
    out = jax.ShapeDtypeStruct(rhs.shape, jnp.float32)
    return pl.pallas_call(
        functools.partial(kernel, parts, lax.axis_size("dom")),
        out_shape=(out, out),
        in_specs=[vmem] * 3 + [smem] * 5,
        out_specs=(vmem, vmem),
        scratch_shapes=[
            pltpu.VMEM((STEPS, PEERS, parts, rows, width), jnp.float32),
            pltpu.VMEM((STEPS, 2, parts, 2, rows, width), jnp.float32),
            pltpu.VMEM((2, PEERS, parts, rows, width), jnp.float32),
            pltpu.VMEM((2, 2, parts, 2, rows, width), jnp.float32),
            pltpu.VMEM((ends, 8, width), jnp.int32),
            pltpu.VMEM((ends, 8, width), jnp.int32),
            pltpu.VMEM((rows_dev, rhs_count, width), jnp.float32),
            pltpu.VMEM((rows_dev, rhs_count, width), jnp.float32),
            pltpu.VMEM((parts, 2, 2, rows, width), jnp.float32),
            pltpu.SMEM((rows_dev,), jnp.int32),
            pltpu.SMEM((rows_dev,), jnp.int32),
            pltpu.SemaphoreType.DMA((2, ends, parts)),
            pltpu.SemaphoreType.DMA((2, ends, parts)),
            pltpu.SemaphoreType.DMA((ends,)),
            pltpu.SemaphoreType.DMA((ends,)),
        ],
        compiler_params=pltpu.CompilerParams(collective_id=0, has_side_effects=True),
        name="sweeps",
    )(coupling, diag_inv, rhs, color, local_target, group_peer, group_list, dom_target)


def solution(mesh):
    placed = (
        P(("dom", "sub"), None, None, None),
        P(("dom", "sub"), None, None),
        P(("dom", "sub"), None, None),
        P(("dom", "sub")),
        P(("dom", "sub"), None),
        P(("dom", "sub"), None),
        P(("dom", "sub"), None, None),
        P(("dom", "sub"), None),
    )
    return jax.shard_map(
        on_device,
        mesh=mesh,
        in_specs=placed,
        out_specs=(P(("dom", "sub"), None, None), P(("dom", "sub"), None, None)),
        check_vma=False,
    )
```

```python
import functools

import jax
import jax.numpy as jnp
from jax import lax
from jax.experimental import pallas as pl
from jax.experimental.pallas import tpu as pltpu
from jax.sharding import PartitionSpec as P

MESH = pl.DeviceIdType.MESH
COLORS = 4
SWEEPS = 2
STEPS = COLORS * SWEEPS
SIDE = 4
OFFSETS = sorted(
    [(dx, dy) for dy in range(SIDE) for dx in range(SIDE) if (dx, dy) != (0, 0)],
    key=lambda o: -(min(o[0], SIDE - o[0]) + min(o[1], SIDE - o[1])),
)
PEERS = len(OFFSETS)
ENDS = PEERS + 2
ITEMS = PEERS + 4
STREAMS = 4


def kernel(
    parts, group, coup_in, diag_in, rhs_in, color_in, ltgt_in, gpeer_in, glist_in, dtgt_in, sol_out, def_out,
    coup, diag, rhs, color, ltgt, gpeer, glist, dtgt,
    recv, send, tag_send, tag_recv, resid, solb, near, jrow, rank,
    in_sem, rsem, ssem, tag_rsem, tag_ssem,
):
    me = lax.axis_index("sub")
    dom = lax.axis_index("dom")
    me_x, me_y = me % SIDE, me // SIDE
    peers = [((me_y + dy) % SIDE) * SIDE + (me_x + dx) % SIDE for dx, dy in OFFSETS]
    above, below = (dom + 1) % group, (dom + group - 1) % group
    devices = [{"sub": q} for q in peers] + [{"dom": above}, {"dom": below}]
    rows_dev, rhs_count, width = rhs.shape
    rows = rhs_count // parts

    barrier = pltpu.get_barrier_semaphore()
    for d in devices:
        pl.semaphore_signal(barrier, inc=1, device_id=d, device_id_type=MESH)
    pairs = [
        (color_in, color), (dtgt_in, dtgt), (glist_in, glist), (rhs_in, rhs), (diag_in, diag),
        (gpeer_in, gpeer), (ltgt_in, ltgt), (coup_in, coup),
    ]
    loads = [pltpu.make_async_copy(src, dst, in_sem.at[n]) for n, (src, dst) in enumerate(pairs)]
    for load in loads:
        load.start()
    solb[...] = jnp.zeros_like(solb)

    loads[0].wait()
    colors = [color[r] for r in range(rows_dev)]
    slots = []
    for c in range(COLORS):
        first, total = jnp.int32(rows_dev - 1), jnp.int32(0)
        for r in reversed(range(rows_dev)):
            hit = colors[r] == c
            first = jnp.where(hit, r, first)
            total = total + jnp.where(hit, r, 0)
        slots += [first, jnp.clip(total - first, 0, rows_dev - 1)]
    for s, j in enumerate(slots):
        jrow[s] = j
    for r in range(rows_dev):
        place = jnp.int32(0)
        for s, j in enumerate(slots):
            place = jnp.where(j == r, s, place)
        rank[r] = place

    def tag_copy(n):
        return pltpu.make_async_remote_copy(
            src_ref=tag_send.at[n], dst_ref=tag_recv.at[n], send_sem=tag_ssem,
            recv_sem=tag_rsem, device_id=devices[n], device_id_type=MESH,
        )

    def all_tags():
        return pltpu.make_async_remote_copy(
            src_ref=tag_send, dst_ref=tag_recv, send_sem=tag_ssem,
            recv_sem=tag_rsem, device_id=devices[0], device_id_type=MESH,
        )

    def copy(t, part, n):
        at = n if n < PEERS else pl.ds(PEERS + 2 * (n - PEERS), 2)
        return pltpu.make_async_remote_copy(
            src_ref=send.at[t % 2, part, at], dst_ref=recv.at[t, part, at], send_sem=ssem.at[t % 2, part],
            recv_sem=rsem.at[t % 2, part], device_id=devices[n], device_id_type=MESH,
        )

    def all_copies(t, part):
        return pltpu.make_async_remote_copy(
            src_ref=send.at[t % 2, part], dst_ref=recv.at[t, part], send_sem=ssem.at[t % 2, part],
            recv_sem=rsem.at[t % 2, part], device_id=devices[0], device_id_type=MESH,
        )

    def pair(c):
        return [2 * (c % COLORS), 2 * (c % COLORS) + 1]

    def gather(t, part, into):
        c = t % COLORS
        span = pl.ds(part * rows, rows)
        targets = [jrow[s] for s in into]
        totals = [resid[s, span, :] for s in into]
        for n in range(ITEMS):
            if n < PEERS:
                line = tag_recv[n, pl.ds(c, 1), :]
            else:
                way, i = (n - PEERS) // 2, (n - PEERS) % 2
                line = tag_recv[PEERS + way, pl.ds(2 * c + i, 1), :]
            tag = jnp.broadcast_to(line, (rows, width))
            item = recv[t, part, n]
            totals = [x - jnp.where(tag == j, item, 0.0) for x, j in zip(totals, targets)]
        for s, x in zip(into, totals):
            resid[s, span, :] = x

    def solve(t, part, first):
        c = t % COLORS
        span = pl.ds(part * rows, rows)
        if not first:
            all_copies(t - 1, part).wait_recv()
            gather(t - 1, part, pair(c))
        changes = []
        for s in pair(c):
            new = jnp.dot(
                resid[s, span, :].astype(jnp.bfloat16), diag[jrow[s]], preferred_element_type=jnp.float32
            )
            changes.append((new - solb[s, span, :]).astype(jnp.bfloat16))
            solb[s, span, :] = new
        owners = [jrow[s] for s in pair(c)]
        if first and part == 0:
            loads[5].wait()
            loads[6].wait()
            loads[7].wait()

        def products(i, k):
            both = jnp.concatenate([coup[owners[i], k], coup[owners[i], k + 1]], axis=1)
            out = jnp.dot(changes[i], both, preferred_element_type=jnp.float32)
            return out[:, :width], out[:, width:]

        terms = [products(i, 2) for i in range(2)]
        wants = [[jnp.full((rows, width), gpeer[k, j], jnp.int32) for k in range(2)] for j in owners]
        if first and part == 0:
            pl.semaphore_wait(barrier, ENDS)
        for n, q in enumerate(peers):
            sums = [
                jnp.where(want[0] == q, term[0], jnp.where(want[1] == q, term[1], 0.0))
                for want, term in zip(wants, terms)
            ]
            send[t % 2, part, n] = sums[0] + sums[1]
            copy(t, part, n).start()
        for i in range(2):
            send[t % 2, part, PEERS + i], send[t % 2, part, PEERS + 2 + i] = products(i, 4)
        for n in range(PEERS, ENDS):
            copy(t, part, n).start()
        for i in range(2):
            near[part, i, 0], near[part, i, 1] = products(i, 0)

    def local(t, part):
        c = t % COLORS
        span = pl.ds(part * rows, rows)
        into = pair(c + 1) + pair(c + 2) + pair(c + 3)
        targets = [jrow[s] for s in into]
        totals = [resid[s, span, :] for s in into]
        for i, s in enumerate(pair(c)):
            for k in range(2):
                tag = jnp.full((rows, width), ltgt[k, jrow[s]], jnp.int32)
                item = near[part, i, k]
                totals = [x - jnp.where(tag == j, item, 0.0) for x, j in zip(totals, targets)]
        for s, x in zip(into, totals):
            resid[s, span, :] = x

    loads[3].wait()
    for s, j in enumerate(slots):
        resid[s] = rhs[j]
    loads[4].wait()
    solve(0, 0, True)

    loads[1].wait()
    loads[2].wait()
    line = lax.broadcasted_iota(jnp.int32, (8, width), 0)
    for n, q in enumerate(peers):
        tile = jnp.full((8, width), -1, jnp.int32)
        for c in range(COLORS):
            tile = jnp.where(line == c, glist[0, c, q], tile)
        tag_send[n] = tile
        tag_copy(n).start()
    for way in range(2):
        tile = jnp.full((8, width), -1, jnp.int32)
        for s, j in enumerate(slots):
            tile = jnp.where(line == s, dtgt[way, j], tile)
        tag_send[PEERS + way] = tile
        tag_copy(PEERS + way).start()

    for part in range(1, parts):
        solve(0, part, True)
    for part in range(parts):
        local(0, part)
    all_tags().wait_recv()

    def step(t, carry):
        for part in range(parts):
            @pl.when(t >= 2)
            def _():
                all_copies(t, part).wait_send()

            solve(t, part, False)
            local(t, part)
            gather(t - 1, part, pair(t + 1) + pair(t + 2))
        return carry

    lax.fori_loop(1, STEPS, step, 0)
    for r in range(rows_dev):
        sol_out[r] = solb[rank[r]]
    last = STEPS - 1
    for part in range(parts):
        all_copies(last, part).wait_recv()
        gather(last, part, pair(0) + pair(1) + pair(2))
    for r in range(rows_dev):
        def_out[r] = resid[rank[r]]
    for part in range(parts):
        all_copies(last - 1, part).wait_send()
        all_copies(last, part).wait_send()
    all_tags().wait_send()


def on_device(coupling, diag_inv, rhs, color, local_target, group_peer, group_list, dom_target):
    rows_dev, rhs_count, width = rhs.shape
    parts, rows = STREAMS, rhs_count // STREAMS
    anywhere, vmem = pl.BlockSpec(memory_space=pl.ANY), pl.BlockSpec(memory_space=pltpu.VMEM)
    ints = [color, local_target.T, group_peer.T, group_list, dom_target.T]
    return pl.pallas_call(
        functools.partial(kernel, parts, lax.axis_size("dom")),
        out_shape=(pltpu.VMEM(rhs.shape, jnp.float32), pltpu.VMEM(rhs.shape, jnp.float32)),
        in_specs=[anywhere] * 8,
        out_specs=(vmem, vmem),
        scratch_shapes=[
            pltpu.VMEM(coupling.shape, coupling.dtype),
            pltpu.VMEM(diag_inv.shape, diag_inv.dtype),
            pltpu.VMEM(rhs.shape, rhs.dtype),
            *[pltpu.SMEM(x.shape, x.dtype) for x in ints],
            pltpu.VMEM((STEPS, parts, ITEMS, rows, width), jnp.float32),
            pltpu.VMEM((2, parts, ITEMS, rows, width), jnp.float32),
            pltpu.VMEM((ENDS, 8, width), jnp.int32),
            pltpu.VMEM((ENDS, 8, width), jnp.int32),
            pltpu.VMEM((rows_dev, rhs_count, width), jnp.float32),
            pltpu.VMEM((rows_dev, rhs_count, width), jnp.float32),
            pltpu.VMEM((parts, 2, 2, rows, width), jnp.float32),
            pltpu.SMEM((rows_dev,), jnp.int32),
            pltpu.SMEM((rows_dev,), jnp.int32),
            pltpu.SemaphoreType.DMA((8,)),
            pltpu.SemaphoreType.DMA((2, parts)),
            pltpu.SemaphoreType.DMA((2, parts)),
            pltpu.SemaphoreType.DMA,
            pltpu.SemaphoreType.DMA,
        ],
        compiler_params=pltpu.CompilerParams(collective_id=0, has_side_effects=True),
        name="sweeps",
    )(coupling, diag_inv, rhs, *ints)


def solution(mesh):
    placed = (
        P(("dom", "sub"), None, None, None),
        P(("dom", "sub"), None, None),
        P(("dom", "sub"), None, None),
        P(("dom", "sub")),
        P(("dom", "sub"), None),
        P(("dom", "sub"), None),
        P(("dom", "sub"), None, None),
        P(("dom", "sub"), None),
    )
    return jax.shard_map(
        on_device,
        mesh=mesh,
        in_specs=placed,
        out_specs=(P(("dom", "sub"), None, None), P(("dom", "sub"), None, None)),
        check_vma=False,
    )
```

```python
import functools

import jax
import jax.numpy as jnp
from jax import lax
from jax.experimental import pallas as pl
from jax.experimental.pallas import tpu as pltpu
from jax.sharding import PartitionSpec as P

MESH = pl.DeviceIdType.MESH
COLORS = 4
SWEEPS = 2
STEPS = COLORS * SWEEPS
SIDE = 4
OFFSETS = sorted(
    [(dx, dy) for dy in range(SIDE) for dx in range(SIDE) if (dx, dy) != (0, 0)],
    key=lambda o: (-min(o[0], SIDE - o[0]) * (3 if min(o[1], SIDE - o[1]) else 2) - 2 * min(o[1], SIDE - o[1])),
)
PEERS = len(OFFSETS)
ENDS = PEERS + 2
ITEMS = PEERS + 4
STREAMS = 4


def kernel(
    parts, group, coup_in, diag_in, rhs_in, color_in, ltgt_in, gpeer_in, glist_in, dtgt_in, sol_out, def_out,
    coup, diag, rhs, color, ltgt, gpeer, glist, dtgt,
    recv, send, tag_send, tag_recv, resid, solb, near, jrow, rank,
    in_sem, rsem, ssem, tag_rsem, tag_ssem,
):
    me = lax.axis_index("sub")
    dom = lax.axis_index("dom")
    me_x, me_y = me % SIDE, me // SIDE
    peers = [((me_y + dy) % SIDE) * SIDE + (me_x + dx) % SIDE for dx, dy in OFFSETS]
    above, below = (dom + 1) % group, (dom + group - 1) % group
    devices = [{"sub": q} for q in peers] + [{"dom": above}, {"dom": below}]
    rows_dev, rhs_count, width = rhs.shape
    rows = rhs_count // parts

    barrier = pltpu.get_barrier_semaphore()
    for d in devices:
        pl.semaphore_signal(barrier, inc=1, device_id=d, device_id_type=MESH)
    pairs = [
        (color_in, color), (dtgt_in, dtgt), (glist_in, glist), (rhs_in, rhs), (diag_in, diag),
        (gpeer_in, gpeer), (ltgt_in, ltgt), (coup_in, coup),
    ]
    loads = [pltpu.make_async_copy(src, dst, in_sem.at[n]) for n, (src, dst) in enumerate(pairs)]
    for load in loads:
        load.start()
    solb[...] = jnp.zeros_like(solb)

    loads[0].wait()
    colors = [color[r] for r in range(rows_dev)]
    slots = []
    for c in range(COLORS):
        first, total = jnp.int32(rows_dev - 1), jnp.int32(0)
        for r in reversed(range(rows_dev)):
            hit = colors[r] == c
            first = jnp.where(hit, r, first)
            total = total + jnp.where(hit, r, 0)
        slots += [first, jnp.clip(total - first, 0, rows_dev - 1)]
    for s, j in enumerate(slots):
        jrow[s] = j
    for r in range(rows_dev):
        place = jnp.int32(0)
        for s, j in enumerate(slots):
            place = jnp.where(j == r, s, place)
        rank[r] = place

    def tag_copy(n):
        return pltpu.make_async_remote_copy(
            src_ref=tag_send.at[n], dst_ref=tag_recv.at[n], send_sem=tag_ssem,
            recv_sem=tag_rsem, device_id=devices[n], device_id_type=MESH,
        )

    def all_tags():
        return pltpu.make_async_remote_copy(
            src_ref=tag_send, dst_ref=tag_recv, send_sem=tag_ssem,
            recv_sem=tag_rsem, device_id=devices[0], device_id_type=MESH,
        )

    def copy(t, part, n):
        at = n if n < PEERS else pl.ds(PEERS + 2 * (n - PEERS), 2)
        return pltpu.make_async_remote_copy(
            src_ref=send.at[t % 2, part, at], dst_ref=recv.at[t, part, at], send_sem=ssem.at[t % 2, part],
            recv_sem=rsem.at[t % 2, part], device_id=devices[n], device_id_type=MESH,
        )

    def all_copies(t, part):
        return pltpu.make_async_remote_copy(
            src_ref=send.at[t % 2, part], dst_ref=recv.at[t, part], send_sem=ssem.at[t % 2, part],
            recv_sem=rsem.at[t % 2, part], device_id=devices[0], device_id_type=MESH,
        )

    def pair(c):
        return [2 * (c % COLORS), 2 * (c % COLORS) + 1]

    def gather(t, part, into):
        c = t % COLORS
        span = pl.ds(part * rows, rows)
        targets = [jrow[s] for s in into]
        totals = [resid[s, span, :] for s in into]
        for n in range(ITEMS):
            if n < PEERS:
                line = tag_recv[n, pl.ds(c, 1), :]
            else:
                way, i = (n - PEERS) // 2, (n - PEERS) % 2
                line = tag_recv[PEERS + way, pl.ds(2 * c + i, 1), :]
            tag = jnp.broadcast_to(line, (rows, width))
            item = recv[t, part, n]
            totals = [x - jnp.where(tag == j, item, 0.0) for x, j in zip(totals, targets)]
        for s, x in zip(into, totals):
            resid[s, span, :] = x

    def solve(t, part, first):
        c = t % COLORS
        span = pl.ds(part * rows, rows)
        if not first:
            all_copies(t - 1, part).wait_recv()
            gather(t - 1, part, pair(c))
        changes = []
        for s in pair(c):
            new = jnp.dot(
                resid[s, span, :].astype(jnp.bfloat16), diag[jrow[s]], preferred_element_type=jnp.float32
            )
            changes.append((new - solb[s, span, :]).astype(jnp.bfloat16))
            solb[s, span, :] = new
        owners = [jrow[s] for s in pair(c)]
        if first and part == 0:
            loads[5].wait()
            loads[6].wait()
            loads[7].wait()

        def products(i, k):
            both = jnp.concatenate([coup[owners[i], k], coup[owners[i], k + 1]], axis=1)
            out = jnp.dot(changes[i], both, preferred_element_type=jnp.float32)
            return out[:, :width], out[:, width:]

        terms = [products(i, 2) for i in range(2)]
        wants = [[jnp.full((rows, width), gpeer[k, j], jnp.int32) for k in range(2)] for j in owners]
        for n, q in enumerate(peers):
            sums = [
                jnp.where(want[0] == q, term[0], jnp.where(want[1] == q, term[1], 0.0))
                for want, term in zip(wants, terms)
            ]
            send[t % 2, part, n] = sums[0] + sums[1]
            if not first:
                copy(t, part, n).start()
        for i in range(2):
            send[t % 2, part, PEERS + i], send[t % 2, part, PEERS + 2 + i] = products(i, 4)
        if not first:
            for n in range(PEERS, ENDS):
                copy(t, part, n).start()
        for i in range(2):
            near[part, i, 0], near[part, i, 1] = products(i, 0)

    def local(t, part):
        c = t % COLORS
        span = pl.ds(part * rows, rows)
        into = pair(c + 1) + pair(c + 2) + pair(c + 3)
        targets = [jrow[s] for s in into]
        totals = [resid[s, span, :] for s in into]
        for i, s in enumerate(pair(c)):
            for k in range(2):
                tag = jnp.full((rows, width), ltgt[k, jrow[s]], jnp.int32)
                item = near[part, i, k]
                totals = [x - jnp.where(tag == j, item, 0.0) for x, j in zip(totals, targets)]
        for s, x in zip(into, totals):
            resid[s, span, :] = x

    loads[3].wait()
    for s, j in enumerate(slots):
        resid[s] = rhs[j]
    loads[4].wait()
    for part in range(parts):
        solve(0, part, True)

    loads[1].wait()
    loads[2].wait()
    line = lax.broadcasted_iota(jnp.int32, (8, width), 0)
    for n, q in enumerate(peers):
        tile = jnp.full((8, width), -1, jnp.int32)
        for c in range(COLORS):
            tile = jnp.where(line == c, glist[0, c, q], tile)
        tag_send[n] = tile
    for way in range(2):
        tile = jnp.full((8, width), -1, jnp.int32)
        for s, j in enumerate(slots):
            tile = jnp.where(line == s, dtgt[way, j], tile)
        tag_send[PEERS + way] = tile

    pl.semaphore_wait(barrier, ENDS)
    for part in range(parts):
        for n in range(ENDS):
            copy(0, part, n).start()
        if part == 0:
            for n in range(ENDS):
                tag_copy(n).start()
    for part in range(parts):
        local(0, part)
    all_tags().wait_recv()

    def step(t, carry):
        for part in range(parts):
            @pl.when(t >= 2)
            def _():
                all_copies(t, part).wait_send()

            solve(t, part, False)
            local(t, part)
            gather(t - 1, part, pair(t + 1) + pair(t + 2))
        return carry

    lax.fori_loop(1, STEPS, step, 0)
    for r in range(rows_dev):
        sol_out[r] = solb[rank[r]]
    last = STEPS - 1
    for part in range(parts):
        all_copies(last, part).wait_recv()
        gather(last, part, pair(0) + pair(1) + pair(2))
    for r in range(rows_dev):
        def_out[r] = resid[rank[r]]
    for part in range(parts):
        all_copies(last - 1, part).wait_send()
        all_copies(last, part).wait_send()
    all_tags().wait_send()


def on_device(coupling, diag_inv, rhs, color, local_target, group_peer, group_list, dom_target):
    rows_dev, rhs_count, width = rhs.shape
    parts, rows = STREAMS, rhs_count // STREAMS
    anywhere, vmem = pl.BlockSpec(memory_space=pl.ANY), pl.BlockSpec(memory_space=pltpu.VMEM)
    ints = [color, local_target.T, group_peer.T, group_list, dom_target.T]
    return pl.pallas_call(
        functools.partial(kernel, parts, lax.axis_size("dom")),
        out_shape=(pltpu.VMEM(rhs.shape, jnp.float32), pltpu.VMEM(rhs.shape, jnp.float32)),
        in_specs=[anywhere] * 8,
        out_specs=(vmem, vmem),
        scratch_shapes=[
            pltpu.VMEM(coupling.shape, coupling.dtype),
            pltpu.VMEM(diag_inv.shape, diag_inv.dtype),
            pltpu.VMEM(rhs.shape, rhs.dtype),
            *[pltpu.SMEM(x.shape, x.dtype) for x in ints],
            pltpu.VMEM((STEPS, parts, ITEMS, rows, width), jnp.float32),
            pltpu.VMEM((2, parts, ITEMS, rows, width), jnp.float32),
            pltpu.VMEM((ENDS, 8, width), jnp.int32),
            pltpu.VMEM((ENDS, 8, width), jnp.int32),
            pltpu.VMEM((rows_dev, rhs_count, width), jnp.float32),
            pltpu.VMEM((rows_dev, rhs_count, width), jnp.float32),
            pltpu.VMEM((parts, 2, 2, rows, width), jnp.float32),
            pltpu.SMEM((rows_dev,), jnp.int32),
            pltpu.SMEM((rows_dev,), jnp.int32),
            pltpu.SemaphoreType.DMA((8,)),
            pltpu.SemaphoreType.DMA((2, parts)),
            pltpu.SemaphoreType.DMA((2, parts)),
            pltpu.SemaphoreType.DMA,
            pltpu.SemaphoreType.DMA,
        ],
        compiler_params=pltpu.CompilerParams(collective_id=0, has_side_effects=True),
        name="sweeps",
    )(coupling, diag_inv, rhs, *ints)


def solution(mesh):
    placed = (
        P(("dom", "sub"), None, None, None),
        P(("dom", "sub"), None, None),
        P(("dom", "sub"), None, None),
        P(("dom", "sub")),
        P(("dom", "sub"), None),
        P(("dom", "sub"), None),
        P(("dom", "sub"), None, None),
        P(("dom", "sub"), None),
    )
    return jax.shard_map(
        on_device,
        mesh=mesh,
        in_specs=placed,
        out_specs=(P(("dom", "sub"), None, None), P(("dom", "sub"), None, None)),
        check_vma=False,
    )
```
